32 devices in a mesh: fsdp: 16 (over z, x, core), tp: 2 (over y).
Axes of the slice: x: 2, y: 2, z: 4, core: 2. Of those that a mesh axis runs over, the one named last changes fastest.
Arguments:
- inputs: float32 [32, 784, 512], P('fsdp', 'tp'), may hold values from -6 to 6
- out_grad: float32 [32, 784, 512], P('fsdp', 'tp'), may hold values from -6 to 6
- vec_params: float32 [6, 512], replicated, as said below
- vec_moments: float32 [2, 6, 512], replicated, as said below
- qv_bias: float32 [2, 512], P(None, 'tp'), may hold values from -4 to 4
- qv_moments: float32 [2, 2, 512], P(None, None, 'tp'), as said below
- rel_table: float32 [169, 16], P(None, 'tp'), may hold values from -6 to 6
- rel_moments: float32 [2, 169, 16], P(None, None, 'tp'), as said below
- hidden_bias: float32 [2048], P('tp'), may hold values from -4 to 4
- hidden_moments: float32 [2, 2048], P(None, 'tp'), as said below
- qkv_weight: float32 [3, 512, 512], P(None, 'fsdp', 'tp'), as said below
- qkv_moments: float32 [2, 3, 512, 512], P(None, None, 'fsdp', 'tp'), as said below
- proj_weight: float32 [512, 512], P('tp', 'fsdp'), may hold values from -0.75 to 0.75
- proj_moments: float32 [2, 512, 512], P(None, 'tp', 'fsdp'), as said below
- up_weight: float32 [512, 2048], P('fsdp', 'tp'), may hold values from -0.25 to 0.25
- up_moments: float32 [2, 512, 2048], P(None, 'fsdp', 'tp'), as said below
- down_weight: float32 [2048, 512], P('tp', 'fsdp'), may hold values from -0.125 to 0.125
- down_moments: float32 [2, 2048, 512], P(None, 'tp', 'fsdp'), as said below
Outputs:
- outputs: float32 [32, 784, 512], P('fsdp', 'tp')
- input_grad: float32 [32, 784, 512], P('fsdp', 'tp')
- vec_grad: float32 [6, 512], replicated
- vec_next: float32 [6, 512], replicated
- vec_moments_next: float32 [2, 6, 512], replicated
- qv_grad: float32 [2, 512], P(None, 'tp')
- qv_next: float32 [2, 512], P(None, 'tp')
- qv_moments_next: float32 [2, 2, 512], P(None, None, 'tp')
- rel_grad: float32 [169, 16], P(None, 'tp')
- rel_next: float32 [169, 16], P(None, 'tp')
- rel_moments_next: float32 [2, 169, 16], P(None, None, 'tp')
- hidden_grad: float32 [2048], P('tp')
- hidden_next: float32 [2048], P('tp')
- hidden_moments_next: float32 [2, 2048], P(None, 'tp')
- qkv_grad: float32 [3, 512, 512], P(None, 'fsdp', 'tp')
- qkv_next: float32 [3, 512, 512], P(None, 'fsdp', 'tp')
- qkv_moments_next: float32 [2, 3, 512, 512], P(None, None, 'fsdp', 'tp')
- proj_grad: float32 [512, 512], P('tp', 'fsdp')
- proj_next: float32 [512, 512], P('tp', 'fsdp')
- proj_moments_next: float32 [2, 512, 512], P(None, 'tp', 'fsdp')
- up_grad: float32 [512, 2048], P('fsdp', 'tp')
- up_next: float32 [512, 2048], P('fsdp', 'tp')
- up_moments_next: float32 [2, 512, 2048], P(None, 'fsdp', 'tp')
- down_grad: float32 [2048, 512], P('tp', 'fsdp')
- down_next: float32 [2048, 512], P('tp', 'fsdp')
- down_moments_next: float32 [2, 2048, 512], P(None, 'tp', 'fsdp')
The draws below stay inside these ranges and needn't reach their ends.
Inputs may be any that keep to these rules, and one draw needn't show every extreme that they name: `vec_params`: a custom draw of gains near one and biases. `qkv_weight`: a custom draw of projection weights. `vec_moments`: index 1 of the leading dimension is positive. `qv_moments`: index 1 of the leading dimension is positive. `rel_moments`: index 1 of the leading dimension is positive. `hidden_moments`: index 1 of the leading dimension is positive. `qkv_moments`: index 1 of the leading dimension is positive. `proj_moments`: index 1 of the leading dimension is positive. `up_moments`: index 1 of the leading dimension is positive. `down_moments`: index 1 of the leading dimension is positive.
All inputs are finite; a program needn't handle non-finite values.
Results may differ from the reference program's by a relative error of at most 0.009.
The reference program's roundings to bfloat16 on the way count: a program that leaves them out, or rounds other values in their place, can miss the bound.
Values may be sent and summed in bfloat16 or wider, within the bound.
No kernel may reach another device: no remote copies, remote signals or barrier semaphores. Data moves between devices by JAX's collectives and lax.ppermute only.
A program may use at most 128 MiB of HBM per device.

```python
import math
import jax
import jax.numpy as jnp
import numpy as np
from jax import lax

D = 512
HEADS = 16
HDIM = 32
FF = 2048
WIN = 7
SIDE = 28
SHIFT = 3
STEP = 10
TABLE = 169
IMAGES = 32


def moment_pair(key, shape):
    scale_guess = float(IMAGES * SIDE * SIDE) ** 0.5
    first_key, second_key = jax.random.split(key)
    first_m = 0.15 * scale_guess * jax.random.normal(first_key, shape, jnp.float32)
    second_m = scale_guess * scale_guess * jnp.exp(jax.random.uniform(second_key, shape, jnp.float32, math.log(0.0003), math.log(0.003)))
    return jnp.stack([first_m, second_m])


def draw_vec_params(key, part):
    gain_key, shift_key = jax.random.split(jax.random.fold_in(key, 11))
    gains = 1.0 + 0.1 * jax.random.normal(gain_key, (2, D), jnp.float32)
    shifts = 0.3 * jax.random.normal(shift_key, (4, D), jnp.float32)
    return jnp.stack([gains[0], shifts[0], gains[1], shifts[1], shifts[2], shifts[3]])


def draw_qkv_weight(key, part):
    base_key = jax.random.fold_in(jax.random.fold_in(key, 23), 0)
    base = jax.random.normal(base_key, (3, D, D), jnp.float32) * D ** (-0.5)
    return base


def draw_vec_moments(key, part):
    return moment_pair(key, (6, D))


def draw_qv_moments(key, part):
    return moment_pair(key, (2, D))


def draw_rel_moments(key, part):
    return moment_pair(key, (TABLE, HEADS))


def draw_hidden_moments(key, part):
    return moment_pair(key, (FF,))


def draw_qkv_moments(key, part):
    return moment_pair(key, (3, D, D))


def draw_proj_moments(key, part):
    return moment_pair(key, (D, D))


def draw_up_moments(key, part):
    return moment_pair(key, (D, FF))


def draw_down_moments(key, part):
    return moment_pair(key, (FF, D))


def block_scale(rng, dims, cuts, least, high):
    level = 1.0
    for axis_at, shards_of in cuts:
        draws = jax.random.uniform(jax.random.fold_in(jax.random.fold_in(rng, 6), axis_at), (shards_of,), jnp.float32, least / len(cuts), high / len(cuts))
        level = level * jnp.repeat(jnp.exp(draws), dims[axis_at] // shards_of).reshape((-1,) + (1,) * (len(dims) - 1 - axis_at))
    return level


def normal_values(key, extent, deviation, bound, cuts=(), dtype=jnp.bfloat16):
    loudness = block_scale(key, extent, cuts, -0.22, 0.18) if cuts else 1.0
    entries = jax.random.normal(key, extent, jnp.float32) * deviation * loudness
    return jnp.minimum(jnp.maximum(entries, -bound), bound).astype(dtype)


def setup_inputs(seed: int = 0) -> dict:
    splits = jax.random.split(jax.random.key(seed), 19)
    return {
        "inputs": normal_values(splits[0], (IMAGES, SIDE * SIDE, D), 1.0, 6.0, ((0, 16), (1, 2)), jnp.float32),
        "out_grad": normal_values(splits[1], (IMAGES, SIDE * SIDE, D), 1.0, 6.0, ((0, 16), (1, 2)), jnp.float32),
        "vec_params": draw_vec_params(jax.random.fold_in(splits[18], 71), 0),
        "vec_moments": draw_vec_moments(jax.random.fold_in(splits[18], 71), 0),
        "qv_bias": normal_values(splits[4], (2, D), 0.3, 4.0, ((1, 2),), jnp.float32),
        "qv_moments": draw_qv_moments(jax.random.fold_in(splits[18], 71), 0),
        "rel_table": normal_values(splits[6], (TABLE, HEADS), 1.0, 6.0, ((1, 2),), jnp.float32),
        "rel_moments": draw_rel_moments(jax.random.fold_in(splits[18], 71), 0),
        "hidden_bias": normal_values(splits[8], (FF,), 0.3, 4.0, ((0, 2),), jnp.float32),
        "hidden_moments": draw_hidden_moments(jax.random.fold_in(splits[18], 71), 0),
        "qkv_weight": draw_qkv_weight(jax.random.fold_in(splits[18], 71), 0),
        "qkv_moments": draw_qkv_moments(jax.random.fold_in(splits[18], 71), 0),
        "proj_weight": normal_values(splits[12], (D, D), (D // 8) ** -0.5, 0.75, ((0, 2), (1, 16)), jnp.float32),
        "proj_moments": draw_proj_moments(jax.random.fold_in(splits[18], 71), 0),
        "up_weight": normal_values(splits[14], (D, FF), D ** -0.5, 0.25, ((0, 16), (1, 2)), jnp.float32),
        "up_moments": draw_up_moments(jax.random.fold_in(splits[18], 71), 0),
        "down_weight": normal_values(splits[16], (FF, D), FF ** -0.5, 0.125, ((0, 2), (1, 16)), jnp.float32),
        "down_moments": draw_down_moments(jax.random.fold_in(splits[18], 71), 0),
    }


norm_eps = 1e-05
mask_fill = -100.0
learn_rate = 0.01
beta_one = 0.9
beta_two = 0.999
adam_eps = 1e-08
weight_decay = 0.05

def window_tables():
    per_side = SIDE // WIN
    positions = np.arange(SIDE)
    region = np.where(positions < SIDE - WIN, 0, np.where(positions < SIDE - SHIFT, 1, 2))
    labels = 3 * region[:, None] + region[None, :]
    labels = labels.reshape(per_side, WIN, per_side, WIN).transpose(0, 2, 1, 3).reshape(per_side * per_side, WIN * WIN)
    masking = np.where(labels[:, :, None] != labels[:, None, :], mask_fill, 0.0).astype(np.float32)
    places = np.arange(WIN * WIN)
    rows_at = places // WIN
    cols_at = places % WIN
    table_index = (rows_at[:, None] - rows_at[None, :] + WIN - 1) * (2 * WIN - 1) + (cols_at[:, None] - cols_at[None, :] + WIN - 1)
    onehot = (table_index.reshape(-1)[:, None] == np.arange(TABLE)[None, :]).astype(np.float32)
    return (jnp.asarray(masking), jnp.asarray(onehot))

def to_windows(values):
    batches, _, channels = values.shape
    per_side = SIDE // WIN
    grid_view = values.reshape(batches, SIDE, SIDE, channels)
    grid_view = jnp.roll(grid_view, (-SHIFT, -SHIFT), axis=(1, 2))
    grid_view = grid_view.reshape(batches, per_side, WIN, per_side, WIN, channels).transpose(0, 1, 3, 2, 4, 5)
    return grid_view.reshape(batches * per_side * per_side, WIN * WIN, channels)

def from_windows(values, batches):
    channels = values.shape[-1]
    per_side = SIDE // WIN
    grid_view = values.reshape(batches, per_side, per_side, WIN, WIN, channels).transpose(0, 1, 3, 2, 4, 5)
    grid_view = grid_view.reshape(batches, SIDE, SIDE, channels)
    grid_view = jnp.roll(grid_view, (SHIFT, SHIFT), axis=(1, 2))
    return grid_view.reshape(batches, SIDE * SIDE, channels)

def norm_fwd(values, scale_row, shift_row):
    center = values - lax.optimization_barrier(jnp.mean(values, axis=-1, keepdims=True))
    spread = lax.optimization_barrier(jnp.mean(center * center, axis=-1, keepdims=True))
    inverse = lax.rsqrt(spread + norm_eps)
    unit_rows = center * inverse
    return (unit_rows * scale_row + shift_row, unit_rows, inverse)

def norm_back(upstream, unit_rows, inverse, scale_row):
    scaled = upstream * scale_row
    return inverse * (scaled - lax.optimization_barrier(jnp.mean(scaled, axis=-1, keepdims=True)) - unit_rows * lax.optimization_barrier(jnp.mean(scaled * unit_rows, axis=-1, keepdims=True)))

def gelu_parts(pre_act):
    cdf_part = 0.5 * (1.0 + lax.erf(pre_act * 0.7071067811865476))
    gelu_slope = cdf_part + pre_act * jnp.exp(-0.5 * pre_act * pre_act) * 0.3989422804014327
    return (pre_act * cdf_part, gelu_slope)

def split_heads(projected, feat_width, query_bias, value_bias):
    scale_qk = HDIM ** (-0.5)
    query_rows = ((projected[:, :feat_width] + query_bias) * scale_qk).astype(jnp.bfloat16)
    key_rows = projected[:, feat_width:2 * feat_width].astype(jnp.bfloat16)
    value_rows = (projected[:, 2 * feat_width:] + value_bias).astype(jnp.bfloat16)
    shaped = (-1, WIN * WIN, feat_width // HDIM, HDIM)
    return (query_rows.reshape(shaped), key_rows.reshape(shaped), value_rows.reshape(shaped))

def attention_scores(query_rows, key_rows, position_bias, masking, batches):
    scores = jnp.einsum('wqhd,wkhd->whqk', query_rows.astype(jnp.float32), key_rows.astype(jnp.float32))
    heads_here = scores.shape[1]
    scores = scores + position_bias[None]
    scores = scores.reshape(batches, -1, heads_here, WIN * WIN, WIN * WIN) + masking[None, :, None]
    return scores.reshape(-1, heads_here, WIN * WIN, WIN * WIN)

def attend_forward(query_rows, key_rows, value_rows, position_bias, masking, batches):
    scores = attention_scores(query_rows, key_rows, position_bias, masking, batches)
    row_top = lax.optimization_barrier(jnp.max(scores, axis=-1, keepdims=True))
    log_total = row_top + jnp.log(lax.optimization_barrier(jnp.sum(jnp.exp(scores - row_top), axis=-1, keepdims=True)))
    soft_weights = jnp.exp(scores - log_total).astype(jnp.bfloat16)
    attended = jnp.einsum('whqk,wkhd->wqhd', soft_weights.astype(jnp.float32), value_rows.astype(jnp.float32))
    attended = attended.astype(jnp.bfloat16)
    return (attended.reshape(-1, attended.shape[2] * HDIM), log_total)

def attend_backward(query_rows, key_rows, value_rows, log_total, grad_att, position_bias, masking, batches):
    scores = attention_scores(query_rows, key_rows, position_bias, masking, batches)
    soft_weights = jnp.exp(scores - log_total)
    soft_rounded = soft_weights.astype(jnp.bfloat16)
    grad_soft = jnp.einsum('wqhd,wkhd->whqk', grad_att.astype(jnp.float32), value_rows.astype(jnp.float32))
    grad_scores = soft_weights * (grad_soft - lax.optimization_barrier(jnp.sum(soft_weights * grad_soft, axis=-1, keepdims=True)))
    grad_rounded = grad_scores.astype(jnp.bfloat16).astype(jnp.float32)
    grad_query = jnp.einsum('whqk,wkhd->wqhd', grad_rounded, key_rows.astype(jnp.float32)) * HDIM ** (-0.5)
    grad_key = jnp.einsum('whqk,wqhd->wkhd', grad_rounded, query_rows.astype(jnp.float32))
    grad_value = jnp.einsum('whqk,wqhd->wkhd', soft_rounded.astype(jnp.float32), grad_att.astype(jnp.float32))
    return (grad_query, grad_key, grad_value, lax.optimization_barrier(jnp.sum(grad_scores, axis=0)))

def adam_update(parameter, gradient, moments, decay_rate):
    first_m = beta_one * moments[0] + (1.0 - beta_one) * gradient
    second_m = beta_two * moments[1] + (1.0 - beta_two) * gradient * gradient
    first_hat = first_m / (1.0 - beta_one ** STEP)
    second_hat = second_m / (1.0 - beta_two ** STEP)
    updated = parameter - learn_rate * (first_hat / (jnp.sqrt(second_hat) + adam_eps) + decay_rate * parameter)
    return (updated, jnp.stack([first_m, second_m]))

def reference(inputs, out_grad, vec_params, vec_moments, qv_bias, qv_moments, rel_table, rel_moments, hidden_bias, hidden_moments, qkv_weight, qkv_moments, proj_weight, proj_moments, up_weight, up_moments, down_weight, down_moments):
    masking, onehot = window_tables()
    joined = qkv_weight.astype(jnp.bfloat16).transpose(1, 0, 2).reshape(D, 3 * D)
    proj_rounded = proj_weight.astype(jnp.bfloat16)
    up_rounded = up_weight.astype(jnp.bfloat16)
    down_rounded = down_weight.astype(jnp.bfloat16)
    position_bias = jnp.dot(onehot, rel_table, precision=lax.Precision.HIGHEST)
    position_bias = position_bias.reshape(WIN * WIN, WIN * WIN, HEADS).transpose(2, 0, 1)

    def image_step(totals, inputs_pair):
        image_block = inputs_pair[0][None]
        cot_block = inputs_pair[1][None]
        first_norm, unit_one, inv_one = norm_fwd(image_block, vec_params[0], vec_params[1])
        windows = to_windows(first_norm.astype(jnp.bfloat16))
        projected = jnp.dot(windows.reshape(-1, D), joined, preferred_element_type=jnp.float32)
        query_rows, key_rows, value_rows = split_heads(projected, D, qv_bias[0], qv_bias[1])
        attended, log_total = attend_forward(query_rows, key_rows, value_rows, position_bias, masking, 1)
        partial_value = jnp.dot(attended, proj_rounded, preferred_element_type=jnp.float32)
        middle = image_block + from_windows(partial_value.reshape(-1, WIN * WIN, D), 1) + vec_params[4]
        second, unit_two, inv_two = norm_fwd(middle, vec_params[2], vec_params[3])
        second_rounded = second.astype(jnp.bfloat16).reshape(-1, D)
        pre_act = jnp.dot(second_rounded, up_rounded, preferred_element_type=jnp.float32) + hidden_bias
        activated, gelu_slope = gelu_parts(pre_act)
        act_rounded = activated.astype(jnp.bfloat16)
        result = middle + jnp.dot(act_rounded, down_rounded, preferred_element_type=jnp.float32).reshape(middle.shape) + vec_params[5]
        cot_rounded = cot_block.astype(jnp.bfloat16).reshape(-1, D)
        grad_down = jnp.dot(act_rounded.T, cot_rounded, preferred_element_type=jnp.float32)
        grad_pre = jnp.dot(cot_rounded, down_rounded.T, preferred_element_type=jnp.float32) * gelu_slope
        grad_pre_rounded = grad_pre.astype(jnp.bfloat16)
        grad_hidden = lax.optimization_barrier(jnp.sum(grad_pre, axis=0))
        grad_up = jnp.dot(second_rounded.T, grad_pre_rounded, preferred_element_type=jnp.float32)
        grad_second = jnp.dot(grad_pre_rounded, up_rounded.T, preferred_element_type=jnp.float32).reshape(middle.shape)
        grad_middle = cot_block + norm_back(grad_second, unit_two, inv_two, vec_params[2])
        grad_windows = to_windows(grad_middle.astype(jnp.bfloat16)).reshape(-1, D)
        grad_proj = jnp.dot(attended.T, grad_windows, preferred_element_type=jnp.float32)
        grad_att = jnp.dot(grad_windows, proj_rounded.T, preferred_element_type=jnp.float32).astype(jnp.bfloat16)
        grad_att = grad_att.reshape(-1, WIN * WIN, HEADS, HDIM)
        grad_query, grad_key, grad_value, grad_position = attend_backward(query_rows, key_rows, value_rows, log_total, grad_att, position_bias, masking, 1)
        grad_rel = jnp.dot(onehot.T, grad_position.transpose(1, 2, 0).reshape(-1, HEADS), precision=lax.Precision.HIGHEST)
        grad_qv = jnp.stack([lax.optimization_barrier(jnp.sum(grad_query.reshape(-1, D), axis=0)), lax.optimization_barrier(jnp.sum(grad_value.reshape(-1, D), axis=0))])
        grad_joined = jnp.concatenate([grad_query.reshape(-1, D), grad_key.reshape(-1, D), grad_value.reshape(-1, D)], axis=1).astype(jnp.bfloat16)
        grad_qkv = jnp.dot(windows.reshape(-1, D).T, grad_joined, preferred_element_type=jnp.float32).reshape(D, 3, D).transpose(1, 0, 2)
        grad_first = from_windows(jnp.dot(grad_joined, joined.T, preferred_element_type=jnp.float32).reshape(-1, WIN * WIN, D), 1)
        grad_block = grad_middle + norm_back(grad_first, unit_one, inv_one, vec_params[0])
        grad_vec = jnp.stack([lax.optimization_barrier(jnp.sum(grad_first * unit_one, axis=(0, 1))), lax.optimization_barrier(jnp.sum(grad_first, axis=(0, 1))), lax.optimization_barrier(jnp.sum(grad_second * unit_two, axis=(0, 1))), lax.optimization_barrier(jnp.sum(grad_second, axis=(0, 1))), lax.optimization_barrier(jnp.sum(grad_middle, axis=(0, 1))), lax.optimization_barrier(jnp.sum(cot_block, axis=(0, 1)))])
        step_grads = (grad_vec, grad_qv, grad_rel, grad_hidden, grad_qkv, grad_proj, grad_up, grad_down)
        totals = jax.tree.map(lambda left_part, right_part: left_part + right_part, totals, step_grads)
        return (totals, (result[0], grad_block[0]))
    start_totals = (jnp.zeros((6, D), jnp.float32), jnp.zeros((2, D), jnp.float32), jnp.zeros((TABLE, HEADS), jnp.float32), jnp.zeros((FF,), jnp.float32), jnp.zeros((3, D, D), jnp.float32), jnp.zeros((D, D), jnp.float32), jnp.zeros((D, FF), jnp.float32), jnp.zeros((FF, D), jnp.float32))
    totals, stacked = lax.scan(image_step, start_totals, (inputs, out_grad))
    vec_grad, qv_grad, rel_grad, hidden_grad, qkv_grad, proj_grad, up_grad, down_grad = totals
    vec_next, vec_moments_next = adam_update(vec_params, vec_grad, vec_moments, 0.0)
    qv_next, qv_moments_next = adam_update(qv_bias, qv_grad, qv_moments, 0.0)
    rel_next, rel_moments_next = adam_update(rel_table, rel_grad, rel_moments, 0.0)
    hidden_next, hidden_moments_next = adam_update(hidden_bias, hidden_grad, hidden_moments, 0.0)
    qkv_next, qkv_moments_next = adam_update(qkv_weight, qkv_grad, qkv_moments, weight_decay)
    proj_next, proj_moments_next = adam_update(proj_weight, proj_grad, proj_moments, weight_decay)
    up_next, up_moments_next = adam_update(up_weight, up_grad, up_moments, weight_decay)
    down_next, down_moments_next = adam_update(down_weight, down_grad, down_moments, weight_decay)
    return (stacked[0], stacked[1], vec_grad, vec_next, vec_moments_next, qv_grad, qv_next, qv_moments_next, rel_grad, rel_next, rel_moments_next, hidden_grad, hidden_next, hidden_moments_next, qkv_grad, qkv_next, qkv_moments_next, proj_grad, proj_next, proj_moments_next, up_grad, up_next, up_moments_next, down_grad, down_next, down_moments_next)
```

```python
import functools

import jax
import jax.numpy as jnp
import numpy as np
from jax import lax
from jax.experimental import pallas as pl
from jax.experimental.pallas import tpu as pltpu
from jax.sharding import PartitionSpec as P

D = 512
HEADS = 16
HDIM = 32
FF = 2048
WIN = 7
SIDE = 28
SHIFT = 3
STEP = 10
TABLE = 169


norm_eps = 1e-05
mask_fill = -100.0
learn_rate = 0.01
beta_one = 0.9
beta_two = 0.999
adam_eps = 1e-08
weight_decay = 0.05


def window_tables():
    per_side = SIDE // WIN
    positions = np.arange(SIDE)
    region = np.where(positions < SIDE - WIN, 0, np.where(positions < SIDE - SHIFT, 1, 2))
    labels = 3 * region[:, None] + region[None, :]
    labels = (
        labels.reshape(per_side, WIN, per_side, WIN)
        .transpose(0, 2, 1, 3)
        .reshape(per_side * per_side, WIN * WIN)
    )
    masking = np.where(labels[:, :, None] != labels[:, None, :], mask_fill, 0.0).astype(np.float32)
    places = np.arange(WIN * WIN)
    rows_at = places // WIN
    cols_at = places % WIN
    table_index = (rows_at[:, None] - rows_at[None, :] + WIN - 1) * (2 * WIN - 1) + (
        cols_at[:, None] - cols_at[None, :] + WIN - 1
    )
    onehot = (table_index.reshape(-1)[:, None] == np.arange(TABLE)[None, :]).astype(np.float32)
    return (jnp.asarray(masking), jnp.asarray(onehot))


def to_windows(values):
    batches, _, channels = values.shape
    per_side = SIDE // WIN
    grid_view = values.reshape(batches, SIDE, SIDE, channels)
    grid_view = jnp.roll(grid_view, (-SHIFT, -SHIFT), axis=(1, 2))
    grid_view = grid_view.reshape(batches, per_side, WIN, per_side, WIN, channels).transpose(
        0, 1, 3, 2, 4, 5
    )
    return grid_view.reshape(batches * per_side * per_side, WIN * WIN, channels)


def from_windows(values, batches):
    channels = values.shape[-1]
    per_side = SIDE // WIN
    grid_view = values.reshape(batches, per_side, per_side, WIN, WIN, channels).transpose(
        0, 1, 3, 2, 4, 5
    )
    grid_view = grid_view.reshape(batches, SIDE, SIDE, channels)
    grid_view = jnp.roll(grid_view, (SHIFT, SHIFT), axis=(1, 2))
    return grid_view.reshape(batches, SIDE * SIDE, channels)


def norm_fwd(values, scale_row, shift_row):
    center = values - jnp.mean(values, axis=-1, keepdims=True)
    spread = jnp.mean(center * center, axis=-1, keepdims=True)
    inverse = lax.rsqrt(spread + norm_eps)
    unit_rows = center * inverse
    return (unit_rows * scale_row + shift_row, unit_rows, inverse)


def norm_back(upstream, unit_rows, inverse, scale_row):
    scaled = upstream * scale_row
    return inverse * (
        scaled
        - jnp.mean(scaled, axis=-1, keepdims=True)
        - unit_rows * jnp.mean(scaled * unit_rows, axis=-1, keepdims=True)
    )


def gelu_parts(pre_act):
    cdf_part = 0.5 * (1.0 + lax.erf(pre_act * 0.7071067811865476))
    gelu_slope = cdf_part + pre_act * jnp.exp(-0.5 * pre_act * pre_act) * 0.3989422804014327
    return (pre_act * cdf_part, gelu_slope)


def split_heads(projected, feat_width, query_bias, value_bias):
    scale_qk = HDIM ** (-0.5)
    query_rows = ((projected[:, :feat_width] + query_bias) * scale_qk).astype(jnp.bfloat16)
    key_rows = projected[:, feat_width : 2 * feat_width].astype(jnp.bfloat16)
    value_rows = (projected[:, 2 * feat_width :] + value_bias).astype(jnp.bfloat16)
    shaped = (-1, WIN * WIN, feat_width // HDIM, HDIM)
    return (query_rows.reshape(shaped), key_rows.reshape(shaped), value_rows.reshape(shaped))


def attention_scores(query_rows, key_rows, position_bias, masking, batches):
    scores = jnp.einsum("wqhd,wkhd->whqk", query_rows, key_rows, preferred_element_type=jnp.float32)
    heads_here = scores.shape[1]
    scores = scores + position_bias[None]
    scores = scores.reshape(batches, -1, heads_here, WIN * WIN, WIN * WIN) + masking[None, :, None]
    return scores.reshape(-1, heads_here, WIN * WIN, WIN * WIN)


def attend_forward(query_rows, key_rows, value_rows, position_bias, masking, batches):
    scores = attention_scores(query_rows, key_rows, position_bias, masking, batches)
    row_top = jnp.max(scores, axis=-1, keepdims=True)
    log_total = row_top + jnp.log(jnp.sum(jnp.exp(scores - row_top), axis=-1, keepdims=True))
    soft_weights = jnp.exp(scores - log_total).astype(jnp.bfloat16)
    attended = jnp.einsum(
        "whqk,wkhd->wqhd", soft_weights, value_rows, preferred_element_type=jnp.float32
    )
    attended = attended.astype(jnp.bfloat16)
    return (attended.reshape(-1, attended.shape[2] * HDIM), log_total)


def attend_backward(
    query_rows, key_rows, value_rows, log_total, grad_att, position_bias, masking, batches
):
    scores = attention_scores(query_rows, key_rows, position_bias, masking, batches)
    soft_weights = jnp.exp(scores - log_total)
    soft_rounded = soft_weights.astype(jnp.bfloat16)
    grad_soft = jnp.einsum(
        "wqhd,wkhd->whqk", grad_att, value_rows, preferred_element_type=jnp.float32
    )
    grad_scores = soft_weights * (
        grad_soft - jnp.sum(soft_weights * grad_soft, axis=-1, keepdims=True)
    )
    grad_rounded = grad_scores.astype(jnp.bfloat16)
    grad_query = jnp.einsum(
        "whqk,wkhd->wqhd", grad_rounded, key_rows, preferred_element_type=jnp.float32
    ) * HDIM ** (-0.5)
    grad_key = jnp.einsum(
        "whqk,wqhd->wkhd", grad_rounded, query_rows, preferred_element_type=jnp.float32
    )
    grad_value = jnp.einsum(
        "whqk,wqhd->wkhd", soft_rounded, grad_att, preferred_element_type=jnp.float32
    )
    return (grad_query, grad_key, grad_value, jnp.sum(grad_scores, axis=0))


def adam_update(parameter, gradient, moments, decay_rate):
    first_m = beta_one * moments[0] + (1.0 - beta_one) * gradient
    second_m = beta_two * moments[1] + (1.0 - beta_two) * gradient * gradient
    first_hat = first_m / (1.0 - beta_one**STEP)
    second_hat = second_m / (1.0 - beta_two**STEP)
    updated = parameter - learn_rate * (
        first_hat / (jnp.sqrt(second_hat) + adam_eps) + decay_rate * parameter
    )
    return (updated, jnp.stack([first_m, second_m]))


def body(
    inputs,
    out_grad,
    vec_params,
    vec_moments,
    qv_bias,
    qv_moments,
    rel_table,
    rel_moments,
    hidden_bias,
    hidden_moments,
    qkv_weight,
    qkv_moments,
    proj_weight,
    proj_moments,
    up_weight,
    up_moments,
    down_weight,
    down_moments,
):
    images, rows_here, feat_width = inputs.shape
    local_width = qv_bias.shape[1]
    heads_here = rel_table.shape[1]
    hidden_here = hidden_bias.shape[0]
    tp_place = lax.axis_index("tp")
    masking, onehot = window_tables()
    qkv_full, proj_full, up_full, down_full = (
        lax.all_gather(qkv_weight.astype(jnp.bfloat16), "fsdp", axis=1, tiled=True),
        lax.all_gather(proj_weight.astype(jnp.bfloat16), "fsdp", axis=1, tiled=True),
        lax.all_gather(up_weight.astype(jnp.bfloat16), "fsdp", axis=0, tiled=True),
        lax.all_gather(down_weight.astype(jnp.bfloat16), "fsdp", axis=1, tiled=True),
    )
    joined = qkv_full.transpose(1, 0, 2).reshape(feat_width, 3 * local_width)
    position_bias = jnp.dot(onehot, rel_table, precision=lax.Precision.HIGHEST)
    position_bias = position_bias.reshape(WIN * WIN, WIN * WIN, heads_here).transpose(2, 0, 1)
    first_norm, unit_one, inv_one = norm_fwd(inputs, vec_params[0], vec_params[1])
    first_all = lax.all_gather(first_norm.astype(jnp.bfloat16), "tp", axis=1, tiled=True)
    windows = to_windows(first_all)
    projected = jnp.dot(windows.reshape(-1, feat_width), joined, preferred_element_type=jnp.float32)
    query_rows, key_rows, value_rows = split_heads(projected, local_width, qv_bias[0], qv_bias[1])
    attended, log_total = attend_forward(
        query_rows, key_rows, value_rows, position_bias, masking, images
    )
    partial_value = jnp.dot(attended, proj_full, preferred_element_type=jnp.float32)
    partial_value = from_windows(partial_value.reshape(-1, WIN * WIN, feat_width), images)
    middle = (
        inputs
        + lax.psum_scatter(partial_value, "tp", scatter_dimension=1, tiled=True)
        + vec_params[4]
    )
    second, unit_two, inv_two = norm_fwd(middle, vec_params[2], vec_params[3])
    second_all = lax.all_gather(second.astype(jnp.bfloat16), "tp", axis=1, tiled=True)
    flat_second = second_all.reshape(-1, feat_width)
    pre_act = jnp.dot(flat_second, up_full, preferred_element_type=jnp.float32) + hidden_bias
    activated, gelu_slope = gelu_parts(pre_act)
    act_rounded = activated.astype(jnp.bfloat16)
    mlp_part = jnp.dot(act_rounded, down_full, preferred_element_type=jnp.float32).reshape(
        images, -1, feat_width
    )
    outputs = (
        middle + lax.psum_scatter(mlp_part, "tp", scatter_dimension=1, tiled=True) + vec_params[5]
    )
    qkv_full, proj_full, up_full, down_full = (
        lax.all_gather(qkv_weight.astype(jnp.bfloat16), "fsdp", axis=1, tiled=True),
        lax.all_gather(proj_weight.astype(jnp.bfloat16), "fsdp", axis=1, tiled=True),
        lax.all_gather(up_weight.astype(jnp.bfloat16), "fsdp", axis=0, tiled=True),
        lax.all_gather(down_weight.astype(jnp.bfloat16), "fsdp", axis=1, tiled=True),
    )
    joined = qkv_full.transpose(1, 0, 2).reshape(feat_width, 3 * local_width)
    cot_all = lax.all_gather(out_grad.astype(jnp.bfloat16), "tp", axis=1, tiled=True).reshape(
        -1, feat_width
    )
    grad_down = jnp.dot(act_rounded.T, cot_all, preferred_element_type=jnp.float32)
    grad_pre = jnp.dot(cot_all, down_full.T, preferred_element_type=jnp.float32) * gelu_slope
    grad_pre_rounded = grad_pre.astype(jnp.bfloat16)
    grad_hidden = jnp.sum(grad_pre, axis=0)
    grad_up = jnp.dot(flat_second.T, grad_pre_rounded, preferred_element_type=jnp.float32)
    second_terms = jnp.dot(grad_pre_rounded, up_full.T, preferred_element_type=jnp.float32).reshape(
        images, -1, feat_width
    )
    grad_second = lax.psum_scatter(second_terms, "tp", scatter_dimension=1, tiled=True)
    grad_middle = out_grad + norm_back(grad_second, unit_two, inv_two, vec_params[2])
    grad_mid_all = lax.all_gather(grad_middle.astype(jnp.bfloat16), "tp", axis=1, tiled=True)
    grad_windows = to_windows(grad_mid_all).reshape(-1, feat_width)
    grad_proj = jnp.dot(attended.T, grad_windows, preferred_element_type=jnp.float32)
    grad_att = jnp.dot(grad_windows, proj_full.T, preferred_element_type=jnp.float32).astype(
        jnp.bfloat16
    )
    grad_att = grad_att.reshape(-1, WIN * WIN, heads_here, HDIM)
    grad_query, grad_key, grad_value, grad_position = attend_backward(
        query_rows, key_rows, value_rows, log_total, grad_att, position_bias, masking, images
    )
    grad_rel = jnp.dot(
        onehot.T,
        grad_position.transpose(1, 2, 0).reshape(-1, heads_here),
        precision=lax.Precision.HIGHEST,
    )
    grad_qv = jnp.stack(
        [
            jnp.sum(grad_query.reshape(-1, local_width), axis=0),
            jnp.sum(grad_value.reshape(-1, local_width), axis=0),
        ]
    )
    grad_joined = jnp.concatenate(
        [
            grad_query.reshape(-1, local_width),
            grad_key.reshape(-1, local_width),
            grad_value.reshape(-1, local_width),
        ],
        axis=1,
    ).astype(jnp.bfloat16)
    grad_qkv = jnp.dot(
        windows.reshape(-1, feat_width).T, grad_joined, preferred_element_type=jnp.float32
    )
    grad_qkv = grad_qkv.reshape(feat_width, 3, local_width).transpose(1, 0, 2)
    first_terms = from_windows(
        jnp.dot(grad_joined, joined.T, preferred_element_type=jnp.float32).reshape(
            -1, WIN * WIN, feat_width
        ),
        images,
    )
    grad_first = lax.psum_scatter(first_terms, "tp", scatter_dimension=1, tiled=True)
    input_grad = grad_middle + norm_back(grad_first, unit_one, inv_one, vec_params[0])
    grad_vec = jnp.stack(
        [
            jnp.sum(grad_first * unit_one, axis=(0, 1)),
            jnp.sum(grad_first, axis=(0, 1)),
            jnp.sum(grad_second * unit_two, axis=(0, 1)),
            jnp.sum(grad_second, axis=(0, 1)),
            jnp.sum(grad_middle, axis=(0, 1)),
            jnp.sum(out_grad, axis=(0, 1)),
        ]
    )
    qv_placed = lax.dynamic_update_slice(
        jnp.zeros((2, D), jnp.float32), grad_qv, (0, tp_place * local_width)
    )
    hidden_placed = lax.dynamic_update_slice(
        jnp.zeros((FF,), jnp.float32), grad_hidden, (tp_place * hidden_here,)
    )
    rel_placed = lax.dynamic_update_slice(
        jnp.zeros((TABLE, HEADS), jnp.float32), grad_rel, (0, tp_place * heads_here)
    )
    vec_grad, qv_summed, hidden_summed, rel_summed = lax.psum(
        (grad_vec, qv_placed, hidden_placed, rel_placed), ("fsdp", "tp")
    )
    qv_grad = lax.dynamic_slice(qv_summed, (0, tp_place * local_width), (2, local_width))
    hidden_grad = lax.dynamic_slice(hidden_summed, (tp_place * hidden_here,), (hidden_here,))
    rel_grad = lax.dynamic_slice(rel_summed, (0, tp_place * heads_here), (TABLE, heads_here))
    qkv_grad, proj_grad, up_grad, down_grad = (
        lax.psum_scatter(grad_qkv, "fsdp", scatter_dimension=1, tiled=True),
        lax.psum_scatter(grad_proj, "fsdp", scatter_dimension=1, tiled=True),
        lax.psum_scatter(grad_up, "fsdp", scatter_dimension=0, tiled=True),
        lax.psum_scatter(grad_down, "fsdp", scatter_dimension=1, tiled=True),
    )
    vec_next, vec_moments_next = adam_update(vec_params, vec_grad, vec_moments, 0.0)
    qv_next, qv_moments_next = adam_update(qv_bias, qv_grad, qv_moments, 0.0)
    rel_next, rel_moments_next = adam_update(rel_table, rel_grad, rel_moments, 0.0)
    hidden_next, hidden_moments_next = adam_update(hidden_bias, hidden_grad, hidden_moments, 0.0)
    qkv_next, qkv_moments_next = adam_update(qkv_weight, qkv_grad, qkv_moments, weight_decay)
    proj_next, proj_moments_next = adam_update(proj_weight, proj_grad, proj_moments, weight_decay)
    up_next, up_moments_next = adam_update(up_weight, up_grad, up_moments, weight_decay)
    down_next, down_moments_next = adam_update(down_weight, down_grad, down_moments, weight_decay)
    return (
        outputs,
        input_grad,
        vec_grad,
        vec_next,
        vec_moments_next,
        qv_grad,
        qv_next,
        qv_moments_next,
        rel_grad,
        rel_next,
        rel_moments_next,
        hidden_grad,
        hidden_next,
        hidden_moments_next,
        qkv_grad,
        qkv_next,
        qkv_moments_next,
        proj_grad,
        proj_next,
        proj_moments_next,
        up_grad,
        up_next,
        up_moments_next,
        down_grad,
        down_next,
        down_moments_next,
    )


AXES = ("fsdp", "tp")
PADC = WIN + 1
WROWS = WIN * PADC
QPAD = 64
GROUP = 4
GLANE = GROUP * HDIM
SLANE = GROUP * QPAD
SCALE = HDIM ** (-0.5)
bf16 = jnp.bfloat16
f32 = jnp.float32
VMEM_LIMIT = 60 * 1024 * 1024


def params_of():
    return pltpu.CompilerParams(vmem_limit_bytes=VMEM_LIMIT)


def dot_nn(a, b):
    return lax.dot_general(a, b, (((1,), (0,)), ((), ())), preferred_element_type=f32)


def dot_nt(a, b):
    return lax.dot_general(a, b, (((1,), (1,)), ((), ())), preferred_element_type=f32)


def dot_tn(a, b):
    return lax.dot_general(a, b, (((0,), (0,)), ((), ())), preferred_element_type=f32)


def swap(values, mask, count):
    return lax.ppermute(values, AXES, [(i, i ^ mask) for i in range(count)])


def tree_sum(values):
    while len(values) > 1:
        values = [values[i] + values[i + 1] for i in range(0, len(values), 2)]
    return values[0]


QUAD = ((0, 0), (0, 1), (1, 0), (1, 1))


def quad_mask(kx, ky):
    return 4 * kx + ky


def gather_pieces(shard, depth, count):
    column = jnp.concatenate([shard] + [swap(shard, 8 * k, count) for k in range(1, depth)], axis=0)
    pieces = []
    for kx, ky in QUAD:
        piece = column if kx + ky == 0 else swap(column, quad_mask(kx, ky), count)
        pieces.append(piece)
    return [(piece, swap(piece, 2, count)) for piece in pieces]


def load_pieces(coord_ref, piece_refs, weights, sems, depth):
    z_at, x_at, c_at, y_at = (coord_ref[0], coord_ref[1], coord_ref[2], coord_ref[3])
    rows = piece_refs[0].shape[0] // depth
    copies = []
    for n, ref in enumerate(piece_refs):
        kx, ky = QUAD[n // 2]
        kc = n % 2
        for kz in range(depth):
            place = (((z_at ^ kz) * 2 + (x_at ^ kx)) * 2 + (c_at ^ kc)) * rows
            copies.append(
                pltpu.make_async_copy(
                    ref.at[pl.ds(kz * rows, rows), :],
                    weights.at[y_at ^ ky, pl.ds(pl.multiple_of(place, rows), rows), :],
                    sems.at[n * depth + kz],
                )
            )
    for copy in copies:
        copy.start()
    for copy in copies:
        copy.wait()


def scatter_sum(keep, send, place, depth, count):
    z_at, x_at, c_at, y_at = place
    both = keep.astype(f32) + swap(send, 2, count).astype(f32)
    tps, _, rows, cols = both.shape
    both = both.reshape(tps, depth, 2, rows, cols)

    def part(kx, ky):
        cut = lax.dynamic_slice(
            both, (y_at ^ ky, 0, x_at ^ kx, 0, 0), (1, depth, 1, rows, cols)
        )
        return cut.reshape(depth, rows, cols)

    parts = []
    for kx, ky in QUAD:
        piece = part(kx, ky)
        parts.append(piece if kx + ky == 0 else swap(piece.astype(bf16), quad_mask(kx, ky), count).astype(f32))
    column = tree_sum(parts)
    parts = []
    for k in range(depth):
        piece = lax.dynamic_slice(column, (z_at ^ k, 0, 0), (1, rows, cols))[0]
        parts.append(piece if k == 0 else swap(piece.astype(bf16), 8 * k, count).astype(f32))
    return tree_sum(parts)


def butterfly(values, depth, count):
    values = values + swap(values, 2, count)
    values = tree_sum([values] + [swap(values, quad_mask(*k), count) for k in QUAD[1:]])
    return tree_sum([values] + [swap(values, 8 * k, count) for k in range(1, depth)])


def window_base(row, col_window):
    per_side = SIDE // WIN
    return (((row // WIN) * per_side + col_window) * WIN + row % WIN) * PADC


def column_runs(col_window):
    start = SHIFT + WIN * col_window
    first = min(WIN, SIDE - start)
    runs = [(start, 0, first)]
    if first < WIN:
        runs.append((0, first, WIN - first))
    return runs


def to_windows_kernel(own_ref, halo_ref, out_ref):
    rows = own_ref.shape[1] // SIDE
    for row in range(rows):
        if row < rows - SHIFT:
            src, off = own_ref, (row + SHIFT) * SIDE
        else:
            src, off = halo_ref, (row - (rows - SHIFT)) * SIDE
        for col_window in range(SIDE // WIN):
            base = window_base(row, col_window)
            for start, at, length in column_runs(col_window):
                out_ref[0, base + at : base + at + length, :] = src[
                    0, off + start : off + start + length, :
                ]
            out_ref[0, base + WIN : base + PADC, :] = jnp.zeros((1, out_ref.shape[2]), f32)


def windows_of(own, halo):
    images, tokens, width = own.shape
    padded = tokens // (WIN * WIN) * WROWS
    out = pl.pallas_call(
        to_windows_kernel,
        grid=(images,),
        in_specs=[
            pl.BlockSpec((1, tokens, width), lambda b: (b, 0, 0)),
            pl.BlockSpec((1, halo.shape[1], width), lambda b: (b, 0, 0)),
        ],
        out_specs=pl.BlockSpec((1, padded, width), lambda b: (b, 0, 0)),
        out_shape=jax.ShapeDtypeStruct((images, padded, width), f32),
        compiler_params=params_of(),
        name="to_windows",
    )(own, halo)
    return out.reshape(images * padded, width)


def from_windows_kernel(in_ref, main_ref, back_ref):
    rows = main_ref.shape[1] // SIDE
    for row in range(rows):
        if row < rows - SHIFT:
            dst, off = main_ref, (row + SHIFT) * SIDE
        else:
            dst, off = back_ref, (row - (rows - SHIFT)) * SIDE
        for col_window in range(SIDE // WIN):
            base = window_base(row, col_window)
            for start, at, length in column_runs(col_window):
                dst[0, off + start : off + start + length, :] = in_ref[
                    0, base + at : base + at + length, :
                ]


def tokens_of(values, images, tokens):
    width = values.shape[1]
    values = values.reshape(images, -1, width)
    padded = values.shape[1]
    halo = SHIFT * SIDE
    return pl.pallas_call(
        from_windows_kernel,
        grid=(images,),
        in_specs=[pl.BlockSpec((1, padded, width), lambda b: (b, 0, 0))],
        out_specs=[
            pl.BlockSpec((1, tokens, width), lambda b: (b, 0, 0)),
            pl.BlockSpec((1, halo, width), lambda b: (b, 0, 0)),
        ],
        out_shape=[
            jax.ShapeDtypeStruct((images, tokens, width), f32),
            jax.ShapeDtypeStruct((images, halo, width), f32),
        ],
        compiler_params=params_of(),
        name="from_windows",
    )(values)


def pad_rows(values):
    return jnp.concatenate(
        [values, jnp.zeros((QPAD - values.shape[0], values.shape[1]), values.dtype)], axis=0
    )


def head_blocks(values):
    padded = pad_rows(values)
    head_of = lax.broadcasted_iota(jnp.int32, padded.shape, 1) // HDIM
    return jnp.concatenate(
        [jnp.where(head_of == h, padded, 0.0) for h in range(GROUP)], axis=0
    ).astype(bf16)


def head_diagonal(blocks):
    head_of = lax.broadcasted_iota(jnp.int32, (WROWS, GLANE), 1) // HDIM
    out = jnp.zeros((WROWS, GLANE), f32)
    for h in range(GROUP):
        out = jnp.where(head_of == h, blocks[h * QPAD : h * QPAD + WROWS], out)
    return out


def attn_fwd_kernel(depth, windows, *refs):
    coord_ref = refs[0]
    piece_refs = refs[1:9]
    x_ref, vec_ref, qb_ref, bias_ref, mask_ref = refs[9:14]
    n1_ref, qkv_ref, lse_ref, o_ref, x1_ref, n2_ref = refs[14:20]
    weights, p3, att, sems = refs[20:]
    width = x_ref.shape[1]
    local = qkv_ref.shape[1] // 6

    @pl.when(pl.program_id(0) == 0)
    def _():
        load_pieces(coord_ref, piece_refs, weights, sems, depth)

    x = x_ref[...]
    n1 = norm_fwd(x, vec_ref[0:1, :], vec_ref[1:2, :])[0].astype(bf16)
    n1_ref[...] = n1
    for t in range(2):
        base = 3 * local * t
        prod = dot_nn(n1, weights[t, :, 0 : 3 * local]) + qb_ref[:, base : base + 3 * local]
        p3[:, base : base + local] = prod[:, :local] * SCALE
        p3[:, base + local : base + 3 * local] = prod[:, local:]
    qkv_ref[...] = p3[...].astype(bf16)
    groups = width // GLANE
    half = local // GLANE

    def one_window(w, carry):
        rows = pl.ds(pl.multiple_of(w * WROWS, 8), WROWS)
        for g in range(groups):
            base = 3 * local * (g // half) + GLANE * (g % half)
            q_blk = head_blocks(p3[rows, base : base + GLANE])
            k_b = pad_rows(p3[rows, base + local : base + local + GLANE]).astype(bf16)
            v_b = pad_rows(p3[rows, base + 2 * local : base + 2 * local + GLANE]).astype(bf16)
            scores = dot_nt(k_b, q_blk)[:WROWS] + bias_ref[g] + mask_ref[w]
            top = jnp.max(scores, axis=0, keepdims=True)
            grown = jnp.exp(scores - top)
            total = jnp.sum(grown, axis=0, keepdims=True)
            lse_ref[w, g : g + 1, :] = top + jnp.log(total)
            soft = pad_rows(grown * (1.0 / total)).astype(bf16)
            att[rows, g * GLANE : (g + 1) * GLANE] = head_diagonal(dot_tn(soft, v_b))
        return carry

    lax.fori_loop(0, windows, one_window, 0)
    o_b = att[...].astype(bf16)
    o_ref[...] = o_b
    x1 = x + vec_ref[4:5, :]
    for t in range(2):
        x1 = x1 + dot_nt(o_b[:, local * t : local * (t + 1)], weights[t, :, 3 * local :])
    x1_ref[...] = x1
    n2_ref[...] = norm_fwd(x1, vec_ref[2:3, :], vec_ref[3:4, :])[0].astype(bf16)


def flat_pieces(pieces):
    return [p for pair in pieces for p in pair]


def smem_spec():
    return pl.BlockSpec(memory_space=pltpu.SMEM)


def any_spec():
    return pl.BlockSpec(memory_space=pl.ANY)


def full_spec(shape):
    return pl.BlockSpec(shape, lambda *_: (0,) * len(shape))


def row_spec(rows, cols):
    return pl.BlockSpec((rows, cols), lambda i: (i, 0))


def attn_forward(coords, pieces, x_win, vec_params, q_bias, bias, masks, depth):
    total, width = x_win.shape
    windows = masks.shape[0] // 2
    block = windows * WROWS
    steps = total // block
    pieces = flat_pieces(pieces)
    cols = pieces[0].shape[1]
    groups = width // GLANE
    return pl.pallas_call(
        lambda *refs: attn_fwd_kernel(depth, windows, *refs),
        grid=(steps,),
        in_specs=[smem_spec()]
        + [any_spec()] * 8
        + [
            row_spec(block, width),
            full_spec(vec_params.shape),
            full_spec(q_bias.shape),
            full_spec(bias.shape),
            pl.BlockSpec((windows,) + masks.shape[1:], lambda i: (i % 2, 0, 0)),
        ],
        out_specs=[
            row_spec(block, width),
            row_spec(block, 3 * width),
            pl.BlockSpec((windows, groups, SLANE), lambda i: (i, 0, 0)),
            row_spec(block, width),
            row_spec(block, width),
            row_spec(block, width),
        ],
        out_shape=[
            jax.ShapeDtypeStruct((total, width), bf16),
            jax.ShapeDtypeStruct((total, 3 * width), bf16),
            jax.ShapeDtypeStruct((total // WROWS, groups, SLANE), f32),
            jax.ShapeDtypeStruct((total, width), bf16),
            jax.ShapeDtypeStruct((total, width), f32),
            jax.ShapeDtypeStruct((total, width), bf16),
        ],
        scratch_shapes=[
            pltpu.VMEM((2, width, cols), bf16),
            pltpu.VMEM((block, 3 * width), f32),
            pltpu.VMEM((block, width), f32),
            pltpu.SemaphoreType.DMA((8 * depth,)),
        ],
        compiler_params=params_of(),
        name="attn_forward",
    )(coords, *pieces, x_win, vec_params, q_bias, bias, masks)


def split_core(grad, core, keep_ref, send_ref, rows):
    blocks = grad.reshape(-1, 2, rows, grad.shape[1])
    even, odd = blocks[:, 0], blocks[:, 1]
    keep_ref[0] = jnp.where(core == 0, even, odd).astype(bf16)
    send_ref[0] = jnp.where(core == 0, odd, even).astype(bf16)


def mlp_kernel(depth, chunk, *refs):
    coord_ref = refs[0]
    piece_refs = refs[1:9]
    n2_ref, og_ref, x1_ref, hb_ref, vec_ref = refs[9:14]
    uk_ref, us_ref, dk_ref, ds_ref, hid_ref, out_ref, gx_ref, gxb_ref, sums_ref = refs[14:23]
    weights, g_b, g_t, n_t, a_b, gz_b, o_acc, g_acc, sems = refs[23:]
    step = pl.program_id(0)
    hidden = weights.shape[2] // 2
    per = hidden // chunk
    t = step // per
    col = (step % per) * chunk
    rows = uk_ref.shape[2]
    core = coord_ref[2]

    @pl.when(step == 0)
    def _():
        load_pieces(coord_ref, piece_refs, weights, sems, depth)
        og = og_ref[...]
        g_b[...] = og.astype(bf16)
        g_t[...] = og.T.astype(bf16)
        n_t[...] = n2_ref[...].astype(f32).T.astype(bf16)
        o_acc[...] = jnp.zeros_like(o_acc)
        g_acc[...] = jnp.zeros_like(g_acc)

    w_up = weights[t, :, pl.ds(pl.multiple_of(col, chunk), chunk)]
    w_dn = weights[t, :, pl.ds(pl.multiple_of(hidden + col, chunk), chunk)]
    hid_bias = hb_ref[:, pl.ds(pl.multiple_of(step * chunk, chunk), chunk)]
    total = n2_ref.shape[0]
    blk = total // 4
    hid_sum = jnp.zeros((1, chunk), f32)
    for r in range(4):
        span = slice(r * blk, (r + 1) * blk)
        pre = dot_nn(n2_ref[span, :], w_up) + hid_bias
        act, slope = gelu_parts(pre)
        act = act.astype(bf16)
        a_b[span, :] = act
        o_acc[span, :] += dot_nt(act, w_dn)
        gz = dot_nn(g_b[span, :], w_dn) * slope
        hid_sum = hid_sum + jnp.sum(gz, axis=0, keepdims=True)
        gz = gz.astype(bf16)
        gz_b[span, :] = gz
        g_acc[span, :] += dot_nt(gz, w_up)
    hid_ref[...] = hid_sum
    split_core(dot_nn(n_t[...], gz_b[...]), core, uk_ref, us_ref, rows)
    split_core(dot_nn(g_t[...], a_b[...]), core, dk_ref, ds_ref, rows)

    @pl.when(step == pl.num_programs(0) - 1)
    def _():
        sums = [jnp.zeros((1, x1_ref.shape[1]), f32) for _ in range(4)]
        for r in range(4):
            span = slice(r * blk, (r + 1) * blk)
            x1 = x1_ref[span, :]
            out_ref[span, :] = x1 + o_acc[span, :] + vec_ref[5:6, :]
            _, unit, inverse = norm_fwd(x1, vec_ref[2:3, :], vec_ref[3:4, :])
            gn = g_acc[span, :]
            og = og_ref[span, :]
            gx = og + norm_back(gn, unit, inverse, vec_ref[2:3, :])
            gx_ref[span, :] = gx
            gxb_ref[span, :] = gx.astype(bf16)
            for n, val in enumerate((gn * unit, gn, gx, og)):
                sums[n] = sums[n] + jnp.sum(val, axis=0, keepdims=True)
        for n in range(4):
            sums_ref[n : n + 1, :] = sums[n]


def mlp_both(coords, pieces, n2, og, x1, hid_bias, vec_params, depth):
    total, width = n2.shape
    pieces = flat_pieces(pieces)
    rows = pieces[0].shape[0] // depth
    cols = pieces[0].shape[1]
    hidden = cols // 2
    chunk = 256
    steps = 2 * hidden // chunk
    per = hidden // chunk
    grad_spec = pl.BlockSpec(
        (1, 2 * depth, rows, chunk), lambda i: (i // per, 0, 0, i % per)
    )
    grad_shape = jax.ShapeDtypeStruct((2, 2 * depth, rows, hidden), bf16)
    return pl.pallas_call(
        lambda *refs: mlp_kernel(depth, chunk, *refs),
        grid=(steps,),
        in_specs=[smem_spec()]
        + [any_spec()] * 8
        + [
            full_spec(n2.shape),
            full_spec(og.shape),
            full_spec(x1.shape),
            full_spec(hid_bias.shape),
            full_spec(vec_params.shape),
        ],
        out_specs=[grad_spec] * 4
        + [
            pl.BlockSpec((1, chunk), lambda i: (0, i)),
            full_spec(x1.shape),
            full_spec(x1.shape),
            full_spec(x1.shape),
            full_spec((4, width)),
        ],
        out_shape=[grad_shape] * 4
        + [
            jax.ShapeDtypeStruct((1, 2 * hidden), f32),
            jax.ShapeDtypeStruct((total, width), f32),
            jax.ShapeDtypeStruct((total, width), f32),
            jax.ShapeDtypeStruct((total, width), bf16),
            jax.ShapeDtypeStruct((4, width), f32),
        ],
        scratch_shapes=[
            pltpu.VMEM((2, width, cols), bf16),
            pltpu.VMEM((total, width), bf16),
            pltpu.VMEM((width, total), bf16),
            pltpu.VMEM((width, total), bf16),
            pltpu.VMEM((total, chunk), bf16),
            pltpu.VMEM((total, chunk), bf16),
            pltpu.VMEM((total, width), f32),
            pltpu.VMEM((total, width), f32),
            pltpu.SemaphoreType.DMA((8 * depth,)),
        ],
        compiler_params=params_of(),
        name="mlp_both",
    )(coords, *pieces, n2, og, x1, hid_bias, vec_params)


def attn_bwd_kernel(depth, windows, *refs):
    coord_ref = refs[0]
    piece_refs = refs[1:9]
    x_ref, gx_ref, gxb_ref, qkv_ref, lse_ref, vec_ref, bias_ref, mask_ref = refs[9:17]
    gqkv_ref, ig_ref, dbias_ref, qv_ref, sums_ref = refs[17:22]
    weights, p3, go, gq, sems = refs[22:]
    width = x_ref.shape[1]
    local = qkv_ref.shape[1] // 6
    first = pl.program_id(0) == 0

    @pl.when(first)
    def _():
        load_pieces(coord_ref, piece_refs, weights, sems, depth)
        dbias_ref[...] = jnp.zeros_like(dbias_ref)
        qv_ref[...] = jnp.zeros_like(qv_ref)
        sums_ref[...] = jnp.zeros_like(sums_ref)

    gxb = gxb_ref[...]
    for t in range(2):
        go[:, local * t : local * (t + 1)] = dot_nn(gxb, weights[t, :, 3 * local :])
    p3[...] = qkv_ref[...].astype(f32)
    groups = width // GLANE
    half = local // GLANE

    def one_window(w, carry):
        rows = pl.ds(pl.multiple_of(w * WROWS, 8), WROWS)
        for g in range(groups):
            base = 3 * local * (g // half) + GLANE * (g % half)
            q_blk = head_blocks(p3[rows, base : base + GLANE])
            k_b = pad_rows(p3[rows, base + local : base + local + GLANE]).astype(bf16)
            v_b = pad_rows(p3[rows, base + 2 * local : base + 2 * local + GLANE]).astype(bf16)
            go_blk = head_blocks(go[rows, g * GLANE : (g + 1) * GLANE])
            scores = dot_nt(k_b, q_blk)[:WROWS] + bias_ref[g] + mask_ref[w]
            soft = jnp.exp(scores - lse_ref[w, g : g + 1, :])
            grad_soft = dot_nt(v_b, go_blk)[:WROWS]
            weighted = soft * grad_soft
            grad_scores = soft * (grad_soft - jnp.sum(weighted, axis=0, keepdims=True))
            dbias_ref[g] += grad_scores
            grad_b = pad_rows(grad_scores).astype(bf16)
            soft_b = pad_rows(soft).astype(bf16)
            gq[rows, base : base + GLANE] = head_diagonal(dot_tn(grad_b, k_b)) * SCALE
            gq[rows, base + local : base + local + GLANE] = dot_nn(grad_b, q_blk)[:WROWS]
            gq[rows, base + 2 * local : base + 2 * local + GLANE] = dot_nn(soft_b, go_blk)[:WROWS]
        return carry

    lax.fori_loop(0, windows, one_window, 0)
    full = gq[...]
    qv_ref[...] += jnp.sum(full, axis=0, keepdims=True)
    full = full.astype(bf16)
    gqkv_ref[...] = full
    gn = dot_nt(full[:, : 3 * local], weights[0, :, : 3 * local]) + dot_nt(
        full[:, 3 * local :], weights[1, :, : 3 * local]
    )
    _, unit, inverse = norm_fwd(x_ref[...], vec_ref[0:1, :], vec_ref[1:2, :])
    ig_ref[...] = gx_ref[...] + norm_back(gn, unit, inverse, vec_ref[0:1, :])
    sums_ref[0:1, :] += jnp.sum(gn * unit, axis=0, keepdims=True)
    sums_ref[1:2, :] += jnp.sum(gn, axis=0, keepdims=True)


def attn_backward(coords, pieces, x_win, gx, gxb, qkv, lse, vec_params, bias, masks, depth):
    total, width = x_win.shape
    windows = masks.shape[0] // 2
    block = windows * WROWS
    steps = total // block
    pieces = flat_pieces(pieces)
    cols = pieces[0].shape[1]
    groups = width // GLANE
    return pl.pallas_call(
        lambda *refs: attn_bwd_kernel(depth, windows, *refs),
        grid=(steps,),
        in_specs=[smem_spec()]
        + [any_spec()] * 8
        + [
            row_spec(block, width),
            row_spec(block, width),
            row_spec(block, width),
            row_spec(block, 3 * width),
            pl.BlockSpec((windows, groups, SLANE), lambda i: (i, 0, 0)),
            full_spec(vec_params.shape),
            full_spec(bias.shape),
            pl.BlockSpec((windows,) + masks.shape[1:], lambda i: (i % 2, 0, 0)),
        ],
        out_specs=[
            row_spec(block, 3 * width),
            row_spec(block, width),
            full_spec(bias.shape),
            full_spec((1, 3 * width)),
            full_spec((2, width)),
        ],
        out_shape=[
            jax.ShapeDtypeStruct((total, 3 * width), bf16),
            jax.ShapeDtypeStruct((total, width), f32),
            jax.ShapeDtypeStruct(bias.shape, f32),
            jax.ShapeDtypeStruct((1, 3 * width), f32),
            jax.ShapeDtypeStruct((2, width), f32),
        ],
        scratch_shapes=[
            pltpu.VMEM((2, width, cols), bf16),
            pltpu.VMEM((block, 3 * width), f32),
            pltpu.VMEM((block, width), f32),
            pltpu.VMEM((block, 3 * width), f32),
            pltpu.SemaphoreType.DMA((8 * depth,)),
        ],
        compiler_params=params_of(),
        name="attn_backward",
    )(coords, *pieces, x_win, gx, gxb, qkv, lse, vec_params, bias, masks)


def dweight_kernel(coord_ref, left_ref, right_ref, keep_ref, send_ref, left_t):
    @pl.when(pl.program_id(0) == 0)
    def _():
        left_t[...] = left_ref[...].astype(f32).T.astype(bf16)

    split_core(
        dot_nn(left_t[...], right_ref[...]), coord_ref[2], keep_ref, send_ref, keep_ref.shape[2]
    )


def dweight(coords, left, right, depth):
    total, width = left.shape
    cols = right.shape[1] // 2
    rows = width // (4 * depth)
    spec = pl.BlockSpec((1, 2 * depth, rows, cols), lambda i: (i, 0, 0, 0))
    shape = jax.ShapeDtypeStruct((2, 2 * depth, rows, cols), bf16)
    return pl.pallas_call(
        dweight_kernel,
        grid=(2,),
        in_specs=[
            smem_spec(),
            full_spec(left.shape),
            pl.BlockSpec((total, cols), lambda i: (0, i)),
        ],
        out_specs=[spec, spec],
        out_shape=[shape, shape],
        scratch_shapes=[pltpu.VMEM((width, total), bf16)],
        compiler_params=params_of(),
        name="dweight",
    )(coords, left, right)


def score_tables(rel_full, y_at, tps):
    heads = rel_full.shape[1]
    key_at = np.arange(WROWS)
    query_at = np.arange(QPAD)
    key_r, key_c = key_at // PADC, key_at % PADC
    query_r, query_c = query_at // PADC, query_at % PADC
    index = (query_r[None, :] - key_r[:, None] + WIN - 1) * (2 * WIN - 1) + (
        query_c[None, :] - key_c[:, None] + WIN - 1
    )
    real = (key_c[:, None] < WIN) & (query_c[None, :] < WIN) & (query_r[None, :] < WIN)
    index = np.where(real, index, -1).astype(np.int32)
    picked = jnp.asarray(index.reshape(-1))
    onehot = (picked[:, None] == lax.broadcasted_iota(jnp.int32, (1, TABLE), 1)).astype(f32)
    bias = lax.dot_general(
        rel_full, onehot, (((0,), (1,)), ((), ())), precision=lax.Precision.HIGHEST
    )
    bias = bias.reshape(heads // GROUP, GROUP, WROWS, QPAD).transpose(0, 2, 1, 3)
    bias = bias.reshape(heads // GROUP, WROWS, SLANE)
    fill = np.where(key_c[:, None] < WIN, 0.0, -1e30).astype(np.float32)
    bias = bias + fill[None]
    per_side = SIDE // WIN
    positions = np.arange(SIDE)
    region = np.where(positions < SIDE - WIN, 0, np.where(positions < SIDE - SHIFT, 1, 2))
    region = region.reshape(per_side, WIN)
    row_of = np.minimum(query_r, WIN - 1)
    col_of = np.minimum(query_c, WIN - 1)
    labels = 3 * region[:, None, row_of] + region[None, :, col_of]
    key_labels = labels[:, :, :WROWS]
    masks = np.where(
        key_labels[:, :, :, None] != labels[:, :, None, :], mask_fill, 0.0
    ).astype(np.float32)
    masks = jnp.asarray(masks.reshape(per_side * per_side, WROWS, QPAD))
    here = per_side * per_side // tps
    masks = lax.dynamic_slice(masks, (y_at * here, 0, 0), (here, WROWS, QPAD))
    return bias, jnp.tile(masks, (1, 1, GROUP)), onehot


def window_body(
    inputs,
    out_grad,
    vec_params,
    vec_moments,
    qv_bias,
    qv_moments,
    rel_table,
    rel_moments,
    hidden_bias,
    hidden_moments,
    qkv_weight,
    qkv_moments,
    proj_weight,
    proj_moments,
    up_weight,
    up_moments,
    down_weight,
    down_moments,
    *,
    depth,
    count,
):
    images, tokens, width = inputs.shape
    local = qv_bias.shape[1]
    heads_here = rel_table.shape[1]
    hidden_here = hidden_bias.shape[0]
    rows_w = qkv_weight.shape[1]
    me = lax.axis_index(AXES)
    place = (me >> 3, (me >> 2) & 1, (me >> 1) & 1, me & 1)
    y_at = place[3]
    coords = jnp.stack(place).astype(jnp.int32)
    halo = SHIFT * SIDE

    shard_a = jnp.concatenate(
        [qkv_weight.transpose(1, 0, 2).reshape(rows_w, 3 * local), proj_weight.T], axis=1
    ).astype(bf16)
    shard_b = jnp.concatenate([up_weight, down_weight.T], axis=1).astype(bf16)
    pieces_a = gather_pieces(shard_a, depth, count)
    halo_x = swap(inputs[:, :halo], 1, count)
    small = jnp.concatenate([qv_bias.reshape(-1), rel_table.reshape(-1), hidden_bias])
    other = swap(small, 1, count)
    low = jnp.where(y_at == 0, small, other)
    high = jnp.where(y_at == 0, other, small)

    def unpack(flat):
        n_qv, n_rel = qv_bias.size, rel_table.size
        return (
            flat[:n_qv].reshape(qv_bias.shape),
            flat[n_qv : n_qv + n_rel].reshape(rel_table.shape),
            flat[n_qv + n_rel :],
        )

    (qv_a, rel_a, hid_a), (qv_b, rel_b, hid_b) = unpack(low), unpack(high)
    rel_full = jnp.concatenate([rel_a, rel_b], axis=1)
    hid_full = jnp.concatenate([hid_a, hid_b])[None]
    zero_k = jnp.zeros((local,), f32)
    q_bias = jnp.concatenate([qv_a[0], zero_k, qv_a[1], qv_b[0], zero_k, qv_b[1]])[None]
    bias, masks, onehot = score_tables(rel_full, y_at, 2)

    x_win = windows_of(inputs, halo_x)
    pieces_b = gather_pieces(shard_b, depth, count)
    halo_g = swap(out_grad[:, :halo], 1, count)
    n1, qkv, lse, att, x1, n2 = attn_forward(
        coords, pieces_a, x_win, vec_params, q_bias, bias, masks, depth
    )
    og_win = windows_of(out_grad, halo_g)
    up_keep, up_send, dn_keep, dn_send, hid_sum, out_win, gx, gxb, sums_two = mlp_both(
        coords, pieces_b, n2, og_win, x1, hid_full, vec_params, depth
    )
    out_main, out_back = tokens_of(out_win, images, tokens)
    outputs = lax.dynamic_update_slice(out_main, swap(out_back, 1, count), (0, 0, 0))
    up_grad = scatter_sum(up_keep, up_send, place, depth, count)
    down_grad = scatter_sum(dn_keep, dn_send, place, depth, count).T
    proj_keep, proj_send = dweight(coords, gxb, att, depth)
    proj_grad = scatter_sum(proj_keep, proj_send, place, depth, count).T
    gqkv, ig_win, dbias, qv_sum, sums_one = attn_backward(
        coords, pieces_a, x_win, gx, gxb, qkv, lse, vec_params, bias, masks, depth
    )
    qkv_keep, qkv_send = dweight(coords, n1, gqkv, depth)
    qkv_grad = scatter_sum(qkv_keep, qkv_send, place, depth, count)
    qkv_grad = qkv_grad.reshape(rows_w, 3, local).transpose(1, 0, 2)
    ig_main, ig_back = tokens_of(ig_win, images, tokens)
    input_grad = lax.dynamic_update_slice(ig_main, swap(ig_back, 1, count), (0, 0, 0))

    heads = rel_full.shape[1]
    by_head = dbias.reshape(heads // GROUP, WROWS, GROUP, QPAD).transpose(0, 2, 1, 3)
    rel_sum = lax.dot_general(
        onehot,
        by_head.reshape(heads, WROWS * QPAD),
        (((0,), (1,)), ((), ())),
        precision=lax.Precision.HIGHEST,
    )
    qv_six = qv_sum.reshape(2, 3, local)
    qv_sum = jnp.stack([qv_six[:, 0].reshape(-1), qv_six[:, 2].reshape(-1)])
    small = jnp.concatenate(
        [
            sums_one.reshape(-1),
            sums_two.reshape(-1),
            qv_sum.reshape(-1),
            rel_sum.reshape(-1),
            hid_sum.reshape(-1),
        ]
    )
    small = butterfly(small, depth, count)
    n_vec, n_qv, n_rel = vec_params.size, qv_sum.size, rel_sum.size
    vec_grad = small[:n_vec].reshape(vec_params.shape)
    qv_full = small[n_vec : n_vec + n_qv].reshape(qv_sum.shape)
    rel_full = small[n_vec + n_qv : n_vec + n_qv + n_rel].reshape(rel_sum.shape)
    hid_full = small[n_vec + n_qv + n_rel :]
    qv_grad = lax.dynamic_slice(qv_full, (0, y_at * local), (2, local))
    rel_grad = lax.dynamic_slice(rel_full, (0, y_at * heads_here), (TABLE, heads_here))
    hidden_grad = lax.dynamic_slice(hid_full, (y_at * hidden_here,), (hidden_here,))
    vec_next, vec_moments_next = adam_update(vec_params, vec_grad, vec_moments, 0.0)
    qv_next, qv_moments_next = adam_update(qv_bias, qv_grad, qv_moments, 0.0)
    rel_next, rel_moments_next = adam_update(rel_table, rel_grad, rel_moments, 0.0)
    hidden_next, hidden_moments_next = adam_update(hidden_bias, hidden_grad, hidden_moments, 0.0)
    qkv_next, qkv_moments_next = adam_update(qkv_weight, qkv_grad, qkv_moments, weight_decay)
    proj_next, proj_moments_next = adam_update(proj_weight, proj_grad, proj_moments, weight_decay)
    up_next, up_moments_next = adam_update(up_weight, up_grad, up_moments, weight_decay)
    down_next, down_moments_next = adam_update(down_weight, down_grad, down_moments, weight_decay)
    return (
        outputs,
        input_grad,
        vec_grad,
        vec_next,
        vec_moments_next,
        qv_grad,
        qv_next,
        qv_moments_next,
        rel_grad,
        rel_next,
        rel_moments_next,
        hidden_grad,
        hidden_next,
        hidden_moments_next,
        qkv_grad,
        qkv_next,
        qkv_moments_next,
        proj_grad,
        proj_next,
        proj_moments_next,
        up_grad,
        up_next,
        up_moments_next,
        down_grad,
        down_next,
        down_moments_next,
    )


def fits_windows(mesh):
    fsdp, tps = mesh.shape["fsdp"], mesh.shape["tp"]
    pow_two = fsdp >= 16 and fsdp & (fsdp - 1) == 0
    return tps == 2 and pow_two and (SIDE // tps) % WIN == 0


def solution(mesh):
    in_specs = (
        P("fsdp", "tp", None),
        P("fsdp", "tp", None),
        P(),
        P(),
        P(None, "tp"),
        P(None, None, "tp"),
        P(None, "tp"),
        P(None, None, "tp"),
        P("tp"),
        P(None, "tp"),
        P(None, "fsdp", "tp"),
        P(None, None, "fsdp", "tp"),
        P("tp", "fsdp"),
        P(None, "tp", "fsdp"),
        P("fsdp", "tp"),
        P(None, "fsdp", "tp"),
        P("tp", "fsdp"),
        P(None, "tp", "fsdp"),
    )
    out_specs = (
        P("fsdp", "tp", None),
        P("fsdp", "tp", None),
        P(),
        P(),
        P(),
        P(None, "tp"),
        P(None, "tp"),
        P(None, None, "tp"),
        P(None, "tp"),
        P(None, "tp"),
        P(None, None, "tp"),
        P("tp"),
        P("tp"),
        P(None, "tp"),
        P(None, "fsdp", "tp"),
        P(None, "fsdp", "tp"),
        P(None, None, "fsdp", "tp"),
        P("tp", "fsdp"),
        P("tp", "fsdp"),
        P(None, "tp", "fsdp"),
        P("fsdp", "tp"),
        P("fsdp", "tp"),
        P(None, "fsdp", "tp"),
        P("tp", "fsdp"),
        P("tp", "fsdp"),
        P(None, "tp", "fsdp"),
    )
    step = body
    if fits_windows(mesh):
        count = mesh.shape["fsdp"] * mesh.shape["tp"]
        step = functools.partial(window_body, depth=mesh.shape["fsdp"] // 4, count=count)
    return jax.shard_map(step, mesh=mesh, in_specs=in_specs, out_specs=out_specs, check_vma=False)
```
